32 devices in a mesh: fx: 8 (over z, x), fy: 4 (over y, core).
Axes of the slice: x: 2, y: 2, z: 4, core: 2. Of those that a mesh axis runs over, the one named last changes fastest.
Arguments:
- right_side: float32 [512, 2048], P(('fx', 'fy'))
- coupling: float32 [512, 11, 4096], P(('fx', 'fy')), may hold values from -0.109375 to 0.109375
- face_columns: int32 [512, 11], P(('fx', 'fy')), may hold values from 0 to 31, as said below
- ghost_lists: int32 [128, 4], P(('fx', 'fy')), may hold values from 0 to 15, as said below
Outputs:
- solution: float32 [512, 2048], P(('fx', 'fy'))
- residual: float32 [512, 2048], P(('fx', 'fy'))
The draws below stay inside these ranges and needn't reach their ends.
Inputs may be any that keep to these rules, and one draw needn't show every extreme that they name: face_columns[f, 0] is f's own index within its block; entries 1 to 6 name other faces of the same block, all distinct and below 16; entries 7 to 10 are distinct and name received faces, 16 + d * 4 + g for the g-th face of group d of the extended list; every received slot of every block is named by some row of that block. `ghost_lists`: each row names 4 distinct faces of its block by local index.
All inputs are finite; a program needn't handle non-finite values.
Results may differ from the reference program's by a relative error of at most 0.0003.
Values sent between devices are 32-bit elements; how exact they have to be, the bound alone decides.
A program may use at most 64 MiB of HBM per device.

```python
import jax
import jax.numpy as jnp
from jax import lax

DOF = 64
NRHS = 32
BLOCKS = 11
OWNED = 7
POWERS = 3
FACE_DEV = 16
GHOST = 4
FACES = 512
N_FX = 8
N_FY = 4


def draw_right_side(key, part):
    keys = jax.random.split(key, 3)
    blocks_total = N_FX * N_FY
    block_id = (jnp.arange(FACES) // FACE_DEV).astype(jnp.float32)
    position = block_id / max(blocks_total - 1, 1) - 0.5
    base = jax.random.normal(keys[0], (FACES, DOF * NRHS), jnp.float32)
    ramp = jnp.exp(position * jnp.log(3.0))
    face_scale = jnp.exp(jax.random.uniform(keys[1], (FACES,), jnp.float32, jnp.log(0.3), jnp.log(3.0)))
    column_scale = jnp.exp(jax.random.uniform(keys[2], (NRHS,), jnp.float32, jnp.log(0.3), jnp.log(3.0)))
    column_scale = jnp.tile(column_scale, DOF)
    return base * (ramp * face_scale)[:, None] * column_scale[None, :]


def draw_face_columns(key, part):
    keys = jax.random.split(key, 3)
    blocks_total = N_FX * N_FY
    local = jnp.arange(FACES) % FACE_DEV
    row_keys = jax.random.split(keys[0], FACES)

    def owned_pick(one_key):
        return jax.random.permutation(one_key, FACE_DEV - 1)[:OWNED - 1]
    owned = jax.vmap(owned_pick)(row_keys)
    owned = owned + (owned >= local[:, None]).astype(owned.dtype)
    block_keys = jax.random.split(keys[1], blocks_total)

    def cover_pick(one_key):
        return jax.random.permutation(one_key, FACE_DEV)
    cover = jax.vmap(cover_pick)(block_keys).reshape(FACES) % (4 * GHOST)
    other_keys = jax.random.split(keys[2], FACES)

    def other_pick(one_key):
        return jax.random.permutation(one_key, 4 * GHOST - 1)[:BLOCKS - OWNED - 1]
    others = jax.vmap(other_pick)(other_keys)
    others = others + (others >= cover[:, None]).astype(others.dtype)
    received = jnp.concatenate([others, cover[:, None]], axis=1) + FACE_DEV
    return jnp.concatenate([local[:, None], owned, received], axis=1).astype(jnp.int32)


def draw_ghost_lists(key, part):
    list_keys = jax.random.split(key, 4 * N_FX * N_FY)

    def list_pick(one_key):
        return jax.random.permutation(one_key, FACE_DEV)[:GHOST]
    return jax.vmap(list_pick)(list_keys).astype(jnp.int32)


def level_of(own_key, shape, pieces, least, largest):
    def one(dim, blocks):
        draws = jax.random.uniform(jax.random.fold_in(jax.random.fold_in(own_key, 6), dim), (blocks,), jnp.float32, least / len(pieces), largest / len(pieces))
        return jnp.repeat(jnp.exp(draws), shape[dim] // blocks).reshape((-1,) + (1,) * (len(shape) - dim - 1))

    level = one(*pieces[0])
    for cut in pieces[1:]:
        level = level * one(*cut)
    return level


def centred(key, dims, deviation, limit, cuts=(), held_as=jnp.bfloat16):
    array = deviation * jax.random.normal(key, dims, jnp.float32)
    if cuts:
        array = array * level_of(key, dims, cuts, -0.22, 0.18)
    return jnp.clip(array, -limit, limit).astype(held_as)


def setup_inputs(seed: int = 0) -> dict:
    seeds = jax.random.split(jax.random.key(seed), 5)
    return {
        "right_side": draw_right_side(jax.random.fold_in(seeds[4], 71), 0),
        "coupling": centred(seeds[1], (FACES, BLOCKS, DOF * DOF), (4 * BLOCKS * DOF) ** -0.5, 0.109375, ((0, 32),), jnp.float32),
        "face_columns": draw_face_columns(jax.random.fold_in(seeds[4], 71), 0),
        "ghost_lists": draw_ghost_lists(jax.random.fold_in(seeds[4], 71), 0),
    }


def extended_grid(field, ghost_lists):
    width = field.shape[1]
    field_grid = field.reshape(N_FX, N_FY, FACE_DEV, width)
    lists = ghost_lists.reshape(N_FX, N_FY, 4, GHOST)

    def select_rows(direction):
        return jnp.take_along_axis(field_grid, lists[:, :, direction, :][..., None], axis=2)
    zero_fx = jnp.zeros((1, N_FY, GHOST, width), jnp.float32)
    zero_fy = jnp.zeros((N_FX, 1, GHOST, width), jnp.float32)
    from_lower_x = jnp.concatenate([zero_fx, select_rows(1)[:-1]], axis=0)
    from_upper_x = jnp.concatenate([select_rows(0)[1:], zero_fx], axis=0)
    from_lower_y = jnp.concatenate([zero_fy, select_rows(3)[:, :-1]], axis=1)
    from_upper_y = jnp.concatenate([select_rows(2)[:, 1:], zero_fy], axis=1)
    return jnp.concatenate([field_grid, from_lower_x, from_upper_x, from_lower_y, from_upper_y], axis=2)

def apply_coupling(field, coupling, face_columns, ghost_lists):
    extended = extended_grid(field, ghost_lists)
    column_grid = face_columns.reshape(N_FX, N_FY, FACE_DEV * BLOCKS)
    block_mats = coupling.reshape(N_FX, N_FY, FACE_DEV, BLOCKS, DOF, DOF)

    def one_row(items):
        ext_row, col_row, mat_row = items
        picked = jnp.take_along_axis(ext_row, col_row[..., None], axis=1)
        picked = picked.reshape(N_FY, FACE_DEV, BLOCKS, DOF, NRHS)
        return jnp.einsum('yfkab,yfkbr->yfar', mat_row, picked, precision=lax.Precision.HIGHEST)
    result = lax.map(one_row, (extended, column_grid, block_mats))
    return result.reshape(FACES, DOF * NRHS)

def solve_small(gram_total):
    count = NRHS
    row_ids = jnp.arange((POWERS + 1) * count)[:, None]
    col_ids = jnp.arange(POWERS * count)[None, :]
    shift_map = ((row_ids == col_ids) | (row_ids == col_ids + count)).astype(jnp.float32)
    first = (row_ids == jnp.arange(count)[None, :]).astype(jnp.float32)
    high = lax.Precision.HIGHEST
    normal_matrix = jnp.dot(shift_map.T, jnp.dot(gram_total, shift_map, precision=high), precision=high)
    right_terms = jnp.dot(shift_map.T, gram_total[:, :count], precision=high)
    factor = jnp.linalg.cholesky(normal_matrix)
    coeffs = jax.scipy.linalg.cho_solve((factor, True), right_terms)
    combo = first - jnp.dot(shift_map, coeffs, precision=high)
    return (coeffs, combo)

def reference(right_side, coupling, face_columns, ghost_lists):
    fields = [right_side]
    for power_index in range(POWERS):
        fields.append(apply_coupling(fields[-1], coupling, face_columns, ghost_lists))
    stacked = jnp.concatenate([item.reshape(FACES * DOF, NRHS) for item in fields], axis=1)
    high = lax.Precision.HIGHEST
    gram_total = jnp.dot(stacked.T.astype(jnp.float32), stacked.astype(jnp.float32), precision=high, preferred_element_type=jnp.float32)
    coeffs, combo = solve_small(gram_total)
    solution = jnp.dot(stacked[:, :POWERS * NRHS], coeffs, precision=high)
    residual = jnp.dot(stacked, combo, precision=high)
    return (solution.reshape(FACES, DOF * NRHS), residual.reshape(FACES, DOF * NRHS))
```

```python
import functools

import jax
import jax.numpy as jnp
from jax import lax
from jax.experimental import pallas as pl
from jax.experimental.pallas import tpu as pltpu
from jax.sharding import PartitionSpec as P

DOF = 64
NRHS = 32
BLOCKS = 11
OWNED = 7
POWERS = 3
LANES = 128
HALF = DOF // 2
GROUPS = LANES // NRHS
MESH = pl.DeviceIdType.MESH
f32 = jnp.float32
bf16 = jnp.bfloat16


def split(x):
    hi = x.astype(bf16).astype(f32)
    return hi, x - hi


def lane_group(rows):
    return lax.broadcasted_iota(jnp.int32, (rows, LANES), 1) // NRHS


def pick(group, parts):
    out = parts[-1]
    for index in range(len(parts) - 2, -1, -1):
        out = jnp.where(group == index, parts[index], out)
    return out


def replicate(group, rolled, source):
    return pick(group, [rolled[(lane - source) % GROUPS] for lane in range(GROUPS)])


def rolls(x):
    return [x] + [pltpu.roll(x, step * NRHS, 1) for step in range(1, GROUPS)]


def product_tile(x, group):
    hi, lo = split(x)
    zero = jnp.zeros_like(x)
    top = pick(group, [hi, zero, lo, zero])
    bottom = pick(group, [zero, hi, zero, lo])
    return top.astype(bf16), bottom.astype(bf16)


def kernel(shape, right_ref, coupling_ref, columns_ref, ghost_ref, sol_ref, res_ref,
           stage, spread, mats, w0, w1, w2, w3, tiles, acc, send_buf, recv_buf,
           zbuf, vbuf, gram_buf, plane_recv, line_recv, final_buf, wide,
           load_sem, send_sem, recv_sem, ps_sem, pr_sem, ls_sem, lr_sem, as_sem, ar_sem):
    n_fx, n_fy, low, faces = shape
    plane = low * n_fy
    high = n_fx // low
    i = lax.axis_index("fx")
    j = lax.axis_index("fy")
    my_low = i % low
    my_high = i // low
    my_rank = my_low * n_fy + j
    fields = [w0, w1, w2, w3]

    def plane_target(offset):
        rank = lax.rem(my_rank + offset, plane)
        return rank, (my_high * low + rank // n_fy, rank % n_fy)

    def line_target(offset):
        place = lax.rem(my_high + offset, high)
        return (place * low + my_low, j)

    routes = [
        (1, i < n_fx - 1, (i + 1, j), i > 0),
        (0, i > 0, (i - 1, j), i < n_fx - 1),
        (3, j < n_fy - 1, (i, j + 1), j > 0),
        (2, j > 0, (i, j - 1), j < n_fy - 1),
    ]

    chunk = faces // 4
    loads = [
        pltpu.make_async_copy(
            coupling_ref.at[pl.ds(part * chunk, chunk)], stage.at[pl.ds(part * chunk, chunk)], load_sem.at[part]
        )
        for part in range(4)
    ]
    for load in loads:
        load.start()

    barrier = pltpu.get_barrier_semaphore()
    for _, has_target, target, _ in routes:
        @pl.when(has_target)
        def _(target=target):
            pl.semaphore_signal(barrier, inc=1, device_id=target, device_id_type=MESH)
    for offset in range(1, plane):
        pl.semaphore_signal(barrier, inc=1, device_id=plane_target(offset)[1], device_id_type=MESH)
    for offset in range(1, high):
        pl.semaphore_signal(barrier, inc=1, device_id=line_target(offset), device_id_type=MESH)

    g8 = lane_group(8)
    g64 = lane_group(DOF)
    g32 = lane_group(HALF)

    for block in range(faces // 8):
        for tile in range(DOF // GROUPS):
            x = right_ref[8 * block:8 * block + 8, tile * LANES:(tile + 1) * LANES]
            moved = rolls(x)
            for q in range(GROUPS):
                wide[0, pl.ds(8 * block * DOF + tile * GROUPS + q, 8, stride=DOF), :] = replicate(g8, moved, q)
    for face in range(faces):
        w0[face] = wide[0, face * DOF:(face + 1) * DOF, :]

    def field_copies(power):
        return [
            pltpu.make_async_remote_copy(
                src_ref=send_buf.at[power, q], dst_ref=recv_buf.at[power, q],
                send_sem=send_sem.at[power, q], recv_sem=recv_sem.at[power, q],
                device_id=routes[q][2], device_id_type=MESH,
            )
            for q in range(4)
        ]

    def send_field(power):
        field = fields[power]
        copies = field_copies(power)
        for q, (row, has_target, _, _) in enumerate(routes):
            picked = [field[ghost_ref[row, g]] for g in range(GROUPS)]
            send_buf[power, q] = pick(g64, picked)
        if power == 0:
            count = sum(jnp.where(route[1], 1, 0) for route in routes) + (plane - 1) + (high - 1)
            pl.semaphore_wait(barrier, count)
        for q, (_, has_target, _, _) in enumerate(routes):
            @pl.when(has_target)
            def _(copy=copies[q]):
                copy.start()
        return copies

    def build_own(power):
        field = fields[power]

        @pl.loop(0, faces)
        def _(face):
            x = field[face]
            top, bottom = product_tile(x, g64)
            tiles[face, 0:DOF] = top
            tiles[face, DOF:2 * DOF] = bottom

    def own_products():
        @pl.loop(0, faces // 4)
        def _(quad):
            for sub in range(4):
                face = quad * 4 + sub
                right = jnp.concatenate([tiles[columns_ref[face, k]] for k in range(OWNED)], axis=0)
                out = jnp.dot(mats[face, :, :OWNED * LANES], right, preferred_element_type=f32)
                acc[face] = out[:HALF] + out[HALF:]

    def far_products(power):
        field = fields[power + 1]

        @pl.loop(0, faces // 4)
        def _(quad):
            for sub in range(4):
                face = quad * 4 + sub
                right = jnp.concatenate(
                    [tiles[columns_ref[face, k]] for k in range(OWNED, BLOCKS)], axis=0
                )
                out = jnp.dot(mats[face, :, OWNED * LANES:], right, preferred_element_type=f32)
                total = acc[face] + (out[:HALF] + out[HALF:])
                total = total + pltpu.roll(total, LANES // 2, 1)
                turned = pltpu.roll(total, NRHS, 1)
                even = g32 % 2 == 0
                field[face, pl.ds(0, HALF, stride=2), :] = jnp.where(even, total, turned)
                field[face, pl.ds(1, HALF, stride=2), :] = jnp.where(even, turned, total)

    def receive_field(power, copies):
        for q, (_, has_target, _, has_source) in enumerate(routes):
            @pl.when(has_source)
            def _(copy=copies[q]):
                copy.wait_recv()

            @pl.when(jnp.logical_not(has_source))
            def _(q=q):
                recv_buf[power, q] = jnp.zeros((DOF, LANES), f32)
            moved = rolls(recv_buf[power, q])
            for g in range(GROUPS):
                top, bottom = product_tile(replicate(g64, moved, g), g64)
                tiles[faces + q * GROUPS + g, 0:DOF] = top
                tiles[faces + q * GROUPS + g, DOF:2 * DOF] = bottom

            @pl.when(has_target)
            def _(copy=copies[q]):
                copy.wait_send()

    def prepare():
        for load in loads:
            load.wait()

        @pl.loop(0, faces)
        def _(face):
            for t in range(HALF):
                spread[pl.ds(t, BLOCKS, stride=HALF), :] = stage[face, :, t * LANES:(t + 1) * LANES]
            for k in range(BLOCKS):
                hi, lo = split(spread[k * HALF:(k + 1) * HALF, :])
                mats[face, 0:HALF, k * LANES:(k + 1) * LANES] = hi.astype(bf16)
                mats[face, HALF:DOF, k * LANES:(k + 1) * LANES] = lo.astype(bf16)

    for power in range(POWERS):
        copies = send_field(power)
        build_own(power)
        if power == 0:
            prepare()
        own_products()
        receive_field(power, copies)
        far_products(power)

    @pl.loop(0, faces)
    def _(face):
        rows = pl.ds(pl.multiple_of(face * DOF, DOF), DOF)
        a, b, c, d = [field[face] for field in fields]
        hi, lo = split(pick(g64, [a + b, b + c, c + d, a]))
        zbuf[rows, :LANES] = hi.astype(bf16)
        zbuf[rows, LANES:] = lo.astype(bf16)

    z = zbuf[...]
    both = lax.dot_general(z, z, (((0,), (0,)), ((), ())), preferred_element_type=f32)
    gram = (both[:LANES, :LANES] + both[LANES:, LANES:]) + (both[:LANES, LANES:] + both[LANES:, :LANES])
    share = LANES // plane
    for rank in range(plane):
        gram_buf[rank] = gram[rank * share:(rank + 1) * share]

    copies = []
    for offset in range(1, plane):
        rank, target = plane_target(offset)
        copy = pltpu.make_async_remote_copy(
            src_ref=gram_buf.at[rank], dst_ref=plane_recv.at[offset], send_sem=ps_sem.at[offset],
            recv_sem=pr_sem.at[offset], device_id=target, device_id_type=MESH)
        copy.start()
        copies.append(copy)

    @pl.loop(0, faces)
    def _(face):
        rows = pl.ds(pl.multiple_of(face * DOF, DOF), DOF)
        hi, lo = split(pick(g64, [field[face] for field in fields]))
        vbuf[rows, :LANES] = hi.astype(bf16)
        vbuf[rows, LANES:] = lo.astype(bf16)

    total = gram_buf[my_rank]
    for offset, copy in enumerate(copies, 1):
        copy.wait_recv()
        total = total + plane_recv[offset]
    line_recv[my_high] = total
    line = []
    for offset in range(1, high):
        copy = pltpu.make_async_remote_copy(
            src_ref=line_recv.at[my_high], dst_ref=line_recv.at[my_high], send_sem=ls_sem.at[offset],
            recv_sem=lr_sem.at[offset], device_id=line_target(offset), device_id_type=MESH)
        copy.start()
        line.append(copy)
    for copy in copies:
        copy.wait_send()
    for copy in line:
        copy.wait_recv()
    total = line_recv[0]
    for place in range(1, high):
        total = total + line_recv[place]
    final_buf[my_rank] = total
    gather = []
    for offset in range(1, plane):
        copy = pltpu.make_async_remote_copy(
            src_ref=final_buf.at[my_rank], dst_ref=final_buf.at[my_rank], send_sem=as_sem.at[offset],
            recv_sem=ar_sem.at[offset], device_id=plane_target(offset)[1], device_id_type=MESH)
        copy.start()
        gather.append(copy)
    for copy in line:
        copy.wait_send()
    for copy in gather:
        copy.wait_recv()

    full = jnp.concatenate([final_buf[rank] for rank in range(plane)], axis=0)
    count = POWERS * NRHS
    tiles = [full[8 * t:8 * t + 8] for t in range(count // 8)]
    sub = lax.broadcasted_iota(jnp.int32, (8, LANES), 0)
    for step in range(count):
        home, inner = step // 8, step % 8
        pivot_row = jnp.broadcast_to(tiles[home][inner:inner + 1, :], (8, LANES))
        pivot = jnp.broadcast_to(pivot_row[:, step:step + 1], (8, LANES))
        scaled = pivot_row / pivot
        for t in range(len(tiles)):
            factor = jnp.broadcast_to(tiles[t][:, step:step + 1], (8, LANES))
            new = tiles[t] - factor * scaled
            tiles[t] = jnp.where(sub == inner, scaled, new) if t == home else new
    solved = jnp.concatenate(tiles, axis=0)
    coeffs = replicate(lane_group(count), rolls(solved), GROUPS - 1)
    none = jnp.zeros((NRHS, LANES), f32)
    row = lax.broadcasted_iota(jnp.int32, (LANES, LANES), 0)
    col = lax.broadcasted_iota(jnp.int32, (LANES, LANES), 1) % NRHS
    first = jnp.where(row == col, 1.0, 0.0)
    padded = jnp.concatenate([coeffs, none], axis=0)
    combo = first - (padded + jnp.concatenate([none, coeffs], axis=0))
    hi, lo = split(jnp.concatenate([padded, combo], axis=1))
    hi, lo = hi.astype(bf16), lo.astype(bf16)
    twice = jnp.concatenate([hi, hi], axis=0)

    @pl.loop(0, faces // 4)
    def _(quad):
        rows = pl.ds(pl.multiple_of(quad * 4 * DOF, 4 * DOF), 4 * DOF)
        left = vbuf[rows, :]
        out = jnp.dot(left, twice, preferred_element_type=f32)
        wide_part = out + jnp.dot(left[:, :LANES], lo, preferred_element_type=f32)
        wide[0, rows, :] = wide_part[:, :LANES]
        wide[1, rows, :] = wide_part[:, LANES:]
    for part, out_ref in enumerate((sol_ref, res_ref)):
        for block in range(faces // 8):
            for tile in range(DOF // GROUPS):
                parts = [
                    wide[part, pl.ds(8 * block * DOF + tile * GROUPS + q, 8, stride=DOF), :] for q in range(GROUPS)
                ]
                out_ref[8 * block:8 * block + 8, tile * LANES:(tile + 1) * LANES] = pick(g8, parts)
    for copy in gather:
        copy.wait_send()


def on_device(shape, right_side, coupling, face_columns, ghost_lists):
    n_fx, n_fy, low, faces = shape
    plane = low * n_fy
    high = n_fx // low
    share = LANES // plane
    rows = faces * DOF
    vmem = pl.BlockSpec(memory_space=pltpu.VMEM)
    smem = pl.BlockSpec(memory_space=pltpu.SMEM)
    dma = pltpu.SemaphoreType.DMA
    out = jax.ShapeDtypeStruct(right_side.shape, f32)
    return pl.pallas_call(
        functools.partial(kernel, shape),
        out_shape=(out, out),
        in_specs=[vmem, pl.BlockSpec(memory_space=pl.ANY), smem, smem],
        out_specs=(vmem, vmem),
        scratch_shapes=[
            pltpu.VMEM(coupling.shape, f32),
            pltpu.VMEM((BLOCKS * HALF, LANES), f32),
            pltpu.VMEM((faces, DOF, BLOCKS * LANES), bf16),
        ]
        + [pltpu.VMEM((faces, DOF, LANES), f32)] * (POWERS + 1)
        + [
            pltpu.VMEM((faces + 4 * GROUPS, LANES, LANES), bf16),
            pltpu.VMEM((faces, HALF, LANES), f32),
            pltpu.VMEM((POWERS, 4, DOF, LANES), f32),
            pltpu.VMEM((POWERS, 4, DOF, LANES), f32),
            pltpu.VMEM((rows, 2 * LANES), bf16),
            pltpu.VMEM((rows, 2 * LANES), bf16),
            pltpu.VMEM((plane, share, LANES), f32),
            pltpu.VMEM((plane, share, LANES), f32),
            pltpu.VMEM((high, share, LANES), f32),
            pltpu.VMEM((plane, share, LANES), f32),
            pltpu.VMEM((2, rows, LANES), f32),
            dma((4,)),
            dma((POWERS, 4)),
            dma((POWERS, 4)),
            dma((plane,)),
            dma((plane,)),
            dma((high,)),
            dma((high,)),
            dma((plane,)),
            dma((plane,)),
        ],
        compiler_params=pltpu.CompilerParams(
            collective_id=0, has_side_effects=True, vmem_limit_bytes=40 * 2**20
        ),
    )(right_side, coupling, face_columns, ghost_lists)


def solution(mesh):
    n_fx, n_fy = mesh.shape["fx"], mesh.shape["fy"]
    low = 1
    while low * low * 4 <= n_fx:
        low *= 2

    def body(right_side, coupling, face_columns, ghost_lists):
        shape = (n_fx, n_fy, low, right_side.shape[0])
        return on_device(shape, right_side, coupling, face_columns, ghost_lists)

    placed = (
        P(("fx", "fy"), None),
        P(("fx", "fy"), None, None),
        P(("fx", "fy"), None),
        P(("fx", "fy"), None),
    )
    return jax.shard_map(
        body,
        mesh=mesh,
        in_specs=placed,
        out_specs=(P(("fx", "fy"), None), P(("fx", "fy"), None)),
        check_vma=False,
    )
```

```python
import functools

import jax
import jax.numpy as jnp
from jax import lax
from jax.experimental import pallas as pl
from jax.experimental.pallas import tpu as pltpu
from jax.sharding import PartitionSpec as P

DOF = 64
NRHS = 32
BLOCKS = 11
OWNED = 7
POWERS = 3
LANES = 128
HALF = DOF // 2
UNROLL = 16
GROUPS = LANES // NRHS
MESH = pl.DeviceIdType.MESH
f32 = jnp.float32
bf16 = jnp.bfloat16


def split(x):
    hi = x.astype(bf16).astype(f32)
    return hi, x - hi


def lane_group(rows):
    return lax.broadcasted_iota(jnp.int32, (rows, LANES), 1) // NRHS


def pick(group, parts):
    out = parts[-1]
    for index in range(len(parts) - 2, -1, -1):
        out = jnp.where(group == index, parts[index], out)
    return out


def replicate(group, rolled, source):
    return pick(group, [rolled[(lane - source) % GROUPS] for lane in range(GROUPS)])


def rolls(x):
    return [x] + [pltpu.roll(x, step * NRHS, 1) for step in range(1, GROUPS)]


def product_tile(x, group):
    hi, lo = split(x)
    zero = jnp.zeros_like(x)
    top = pick(group, [hi, zero, lo, zero])
    bottom = pick(group, [zero, hi, zero, lo])
    return top.astype(bf16), bottom.astype(bf16)


def kernel(shape, right_ref, coupling_ref, columns_ref, ghost_ref, sol_ref, res_ref,
           stage, spread, mats, w0, w1, w2, w3, tiles, acc, send_buf, recv_buf,
           zbuf, vbuf, gram_buf, plane_recv, line_recv, final_buf, wide,
           load_sem, send_sem, recv_sem, ps_sem, pr_sem, ls_sem, lr_sem, as_sem, ar_sem):
    n_fx, n_fy, low, faces = shape
    plane = low * n_fy
    high = n_fx // low
    i = lax.axis_index("fx")
    j = lax.axis_index("fy")
    my_low = i % low
    my_high = i // low
    my_rank = my_low * n_fy + j
    fields = [w0, w1, w2, w3]

    def plane_target(offset):
        rank = lax.rem(my_rank + offset, plane)
        return rank, (my_high * low + rank // n_fy, rank % n_fy)

    def line_target(offset):
        place = lax.rem(my_high + offset, high)
        return (place * low + my_low, j)

    routes = [
        (1, i < n_fx - 1, (i + 1, j), i > 0),
        (0, i > 0, (i - 1, j), i < n_fx - 1),
        (3, j < n_fy - 1, (i, j + 1), j > 0),
        (2, j > 0, (i, j - 1), j < n_fy - 1),
    ]

    loads = [pltpu.make_async_copy(coupling_ref.at[k], stage.at[k], load_sem.at[k]) for k in range(BLOCKS)]
    for load in loads:
        load.start()

    barrier = pltpu.get_barrier_semaphore()
    for _, has_target, target, _ in routes:
        @pl.when(has_target)
        def _(target=target):
            pl.semaphore_signal(barrier, inc=1, device_id=target, device_id_type=MESH)
    for offset in range(1, plane):
        pl.semaphore_signal(barrier, inc=1, device_id=plane_target(offset)[1], device_id_type=MESH)
    for offset in range(1, high):
        pl.semaphore_signal(barrier, inc=1, device_id=line_target(offset), device_id_type=MESH)

    g8 = lane_group(8)
    g64 = lane_group(DOF)
    g32 = lane_group(HALF)

    for block in range(faces // 8):
        for tile in range(DOF // GROUPS):
            x = right_ref[8 * block:8 * block + 8, tile * LANES:(tile + 1) * LANES]
            moved = rolls(x)
            for q in range(GROUPS):
                wide[0, pl.ds(8 * block * DOF + tile * GROUPS + q, 8, stride=DOF), :] = replicate(g8, moved, q)
    for face in range(faces):
        w0[face] = wide[0, face * DOF:(face + 1) * DOF, :]

    def field_copies(power):
        return [
            pltpu.make_async_remote_copy(
                src_ref=send_buf.at[power, q], dst_ref=recv_buf.at[power, q],
                send_sem=send_sem.at[power, q], recv_sem=recv_sem.at[power, q],
                device_id=routes[q][2], device_id_type=MESH,
            )
            for q in range(4)
        ]

    def send_field(power):
        field = fields[power]
        copies = field_copies(power)
        for q, (row, has_target, _, _) in enumerate(routes):
            picked = [field[ghost_ref[row, g]] for g in range(GROUPS)]
            send_buf[power, q] = pick(g64, picked)
        if power == 0:
            count = sum(jnp.where(route[1], 1, 0) for route in routes) + (plane - 1) + (high - 1)
            pl.semaphore_wait(barrier, count)
        for q, (_, has_target, _, _) in enumerate(routes):
            @pl.when(has_target)
            def _(copy=copies[q]):
                copy.start()
        return copies

    def build_own(power):
        field = fields[power]

        @pl.loop(0, faces)
        def _(face):
            x = field[face]
            top, bottom = product_tile(x, g64)
            tiles[face, 0:DOF] = top
            tiles[face, DOF:2 * DOF] = bottom

    def own_products():
        @pl.loop(0, faces // UNROLL)
        def _(part):
            for sub in range(UNROLL):
                face = part * UNROLL + sub
                right = jnp.concatenate([tiles[columns_ref[face, k]] for k in range(OWNED)], axis=0)
                out = jnp.dot(mats[face, :, :OWNED * LANES], right, preferred_element_type=f32)
                acc[face] = out[:HALF] + out[HALF:]

    def far_products(power):
        field = fields[power + 1]

        @pl.loop(0, faces // UNROLL)
        def _(part):
            for sub in range(UNROLL):
                face = part * UNROLL + sub
                right = jnp.concatenate(
                    [tiles[columns_ref[face, k]] for k in range(OWNED, BLOCKS)], axis=0
                )
                out = jnp.dot(mats[face, :, OWNED * LANES:], right, preferred_element_type=f32)
                total = acc[face] + (out[:HALF] + out[HALF:])
                total = total + pltpu.roll(total, LANES // 2, 1)
                turned = pltpu.roll(total, NRHS, 1)
                even = g32 % 2 == 0
                field[face, pl.ds(0, HALF, stride=2), :] = jnp.where(even, total, turned)
                field[face, pl.ds(1, HALF, stride=2), :] = jnp.where(even, turned, total)

    def receive_field(power, copies):
        for q, (_, has_target, _, has_source) in enumerate(routes):
            @pl.when(has_source)
            def _(copy=copies[q]):
                copy.wait_recv()

            @pl.when(jnp.logical_not(has_source))
            def _(q=q):
                recv_buf[power, q] = jnp.zeros((DOF, LANES), f32)
            moved = rolls(recv_buf[power, q])
            for g in range(GROUPS):
                top, bottom = product_tile(replicate(g64, moved, g), g64)
                tiles[faces + q * GROUPS + g, 0:DOF] = top
                tiles[faces + q * GROUPS + g, DOF:2 * DOF] = bottom

            @pl.when(has_target)
            def _(copy=copies[q]):
                copy.wait_send()

    def prepare():
        for k in range(BLOCKS):
            loads[k].wait()
            for block in range(faces // 8):
                for t in range(HALF):
                    spread[k % 2, pl.ds(8 * block * HALF + t, 8, stride=HALF), :] = stage[
                        k, 8 * block:8 * block + 8, t * LANES:(t + 1) * LANES]
            for face in range(faces):
                hi, lo = split(spread[k % 2, face * HALF:(face + 1) * HALF, :])
                mats[face, 0:HALF, k * LANES:(k + 1) * LANES] = hi.astype(bf16)
                mats[face, HALF:DOF, k * LANES:(k + 1) * LANES] = lo.astype(bf16)

    for power in range(POWERS):
        copies = send_field(power)
        build_own(power)
        if power == 0:
            prepare()
        own_products()
        receive_field(power, copies)
        far_products(power)

    @pl.loop(0, faces)
    def _(face):
        rows = pl.ds(pl.multiple_of(face * DOF, DOF), DOF)
        a, b, c, d = [field[face] for field in fields]
        hi, lo = split(pick(g64, [a + b, b + c, c + d, a]))
        zbuf[rows, :LANES] = hi.astype(bf16)
        zbuf[rows, LANES:] = lo.astype(bf16)

    z = zbuf[...]
    both = lax.dot_general(z, z, (((0,), (0,)), ((), ())), preferred_element_type=f32)
    gram = (both[:LANES, :LANES] + both[LANES:, LANES:]) + (both[:LANES, LANES:] + both[LANES:, :LANES])
    share = LANES // plane
    for rank in range(plane):
        gram_buf[rank] = gram[rank * share:(rank + 1) * share]

    copies = []
    for offset in range(1, plane):
        rank, target = plane_target(offset)
        copy = pltpu.make_async_remote_copy(
            src_ref=gram_buf.at[rank], dst_ref=plane_recv.at[offset], send_sem=ps_sem.at[offset],
            recv_sem=pr_sem.at[offset], device_id=target, device_id_type=MESH)
        copy.start()
        copies.append(copy)

    @pl.loop(0, faces)
    def _(face):
        rows = pl.ds(pl.multiple_of(face * DOF, DOF), DOF)
        hi, lo = split(pick(g64, [field[face] for field in fields]))
        vbuf[rows, :LANES] = hi.astype(bf16)
        vbuf[rows, LANES:] = lo.astype(bf16)

    total = gram_buf[my_rank]
    for offset, copy in enumerate(copies, 1):
        copy.wait_recv()
        total = total + plane_recv[offset]
    line_recv[my_high] = total
    line = []
    for offset in range(1, high):
        copy = pltpu.make_async_remote_copy(
            src_ref=line_recv.at[my_high], dst_ref=line_recv.at[my_high], send_sem=ls_sem.at[offset],
            recv_sem=lr_sem.at[offset], device_id=line_target(offset), device_id_type=MESH)
        copy.start()
        line.append(copy)
    for copy in copies:
        copy.wait_send()
    for copy in line:
        copy.wait_recv()
    total = line_recv[0]
    for place in range(1, high):
        total = total + line_recv[place]
    final_buf[my_rank] = total
    gather = []
    for offset in range(1, plane):
        copy = pltpu.make_async_remote_copy(
            src_ref=final_buf.at[my_rank], dst_ref=final_buf.at[my_rank], send_sem=as_sem.at[offset],
            recv_sem=ar_sem.at[offset], device_id=plane_target(offset)[1], device_id_type=MESH)
        copy.start()
        gather.append(copy)
    for copy in line:
        copy.wait_send()
    for copy in gather:
        copy.wait_recv()

    full = jnp.concatenate([final_buf[rank] for rank in range(plane)], axis=0)
    count = POWERS * NRHS
    tiles = [full[8 * t:8 * t + 8] for t in range(count // 8)]
    sub = lax.broadcasted_iota(jnp.int32, (8, LANES), 0)

    def across(x, lane):
        return jnp.broadcast_to(x[:, lane:lane + 1], (8, LANES))

    def down(x, row):
        return jnp.broadcast_to(x[row:row + 1, :], (8, LANES))

    for home in range(len(tiles)):
        mine = tiles[home]
        cols = [across(mine, 8 * home + c) for c in range(8)]
        for step in range(8):
            inverse = 1.0 / down(cols[step], step)
            here = sub == step
            factor = cols[step]
            scaled = down(mine, step) * inverse
            mine = jnp.where(here, scaled, mine - factor * scaled)
            for c in range(step + 1, 8):
                scaled = down(cols[c], step) * inverse
                cols[c] = jnp.where(here, scaled, cols[c] - factor * scaled)
        tiles[home] = mine
        rows8 = [down(mine, c) for c in range(8)]
        order = [t % len(tiles) for t in range(home + 1, home + len(tiles))]
        for t in order:
            terms = [across(tiles[t], 8 * home + c) * rows8[c] for c in range(8)]
            while len(terms) > 1:
                terms = [terms[k] + terms[k + 1] for k in range(0, len(terms), 2)]
            tiles[t] = tiles[t] - terms[0]
    solved = jnp.concatenate(tiles, axis=0)
    coeffs = replicate(lane_group(count), rolls(solved), GROUPS - 1)
    none = jnp.zeros((NRHS, LANES), f32)
    row = lax.broadcasted_iota(jnp.int32, (LANES, LANES), 0)
    col = lax.broadcasted_iota(jnp.int32, (LANES, LANES), 1) % NRHS
    first = jnp.where(row == col, 1.0, 0.0)
    padded = jnp.concatenate([coeffs, none], axis=0)
    combo = first - (padded + jnp.concatenate([none, coeffs], axis=0))
    hi, lo = split(jnp.concatenate([padded, combo], axis=1))
    hi, lo = hi.astype(bf16), lo.astype(bf16)
    twice = jnp.concatenate([hi, hi], axis=0)

    @pl.loop(0, faces // 4)
    def _(quad):
        rows = pl.ds(pl.multiple_of(quad * 4 * DOF, 4 * DOF), 4 * DOF)
        left = vbuf[rows, :]
        out = jnp.dot(left, twice, preferred_element_type=f32)
        wide_part = out + jnp.dot(left[:, :LANES], lo, preferred_element_type=f32)
        wide[0, rows, :] = wide_part[:, :LANES]
        wide[1, rows, :] = wide_part[:, LANES:]
    for part, out_ref in enumerate((sol_ref, res_ref)):
        for block in range(faces // 8):
            for tile in range(DOF // GROUPS):
                parts = [
                    wide[part, pl.ds(8 * block * DOF + tile * GROUPS + q, 8, stride=DOF), :] for q in range(GROUPS)
                ]
                out_ref[8 * block:8 * block + 8, tile * LANES:(tile + 1) * LANES] = pick(g8, parts)
    for copy in gather:
        copy.wait_send()


def on_device(shape, right_side, coupling, face_columns, ghost_lists):
    n_fx, n_fy, low, faces = shape
    plane = low * n_fy
    high = n_fx // low
    share = LANES // plane
    rows = faces * DOF
    vmem = pl.BlockSpec(memory_space=pltpu.VMEM)
    smem = pl.BlockSpec(memory_space=pltpu.SMEM)
    dma = pltpu.SemaphoreType.DMA
    out = jax.ShapeDtypeStruct(right_side.shape, f32)
    return pl.pallas_call(
        functools.partial(kernel, shape),
        out_shape=(out, out),
        in_specs=[vmem, pl.BlockSpec(memory_space=pltpu.HBM), smem, smem],
        out_specs=(vmem, vmem),
        scratch_shapes=[
            pltpu.VMEM(coupling.shape, f32),
            pltpu.VMEM((2, faces * HALF, LANES), f32),
            pltpu.VMEM((faces, DOF, BLOCKS * LANES), bf16),
        ]
        + [pltpu.VMEM((faces, DOF, LANES), f32)] * (POWERS + 1)
        + [
            pltpu.VMEM((faces + 4 * GROUPS, LANES, LANES), bf16),
            pltpu.VMEM((faces, HALF, LANES), f32),
            pltpu.VMEM((POWERS, 4, DOF, LANES), f32),
            pltpu.VMEM((POWERS, 4, DOF, LANES), f32),
            pltpu.VMEM((rows, 2 * LANES), bf16),
            pltpu.VMEM((rows, 2 * LANES), bf16),
            pltpu.VMEM((plane, share, LANES), f32),
            pltpu.VMEM((plane, share, LANES), f32),
            pltpu.VMEM((high, share, LANES), f32),
            pltpu.VMEM((plane, share, LANES), f32),
            pltpu.VMEM((2, rows, LANES), f32),
            dma((BLOCKS,)),
            dma((POWERS, 4)),
            dma((POWERS, 4)),
            dma((plane,)),
            dma((plane,)),
            dma((high,)),
            dma((high,)),
            dma((plane,)),
            dma((plane,)),
        ],
        compiler_params=pltpu.CompilerParams(
            collective_id=0, has_side_effects=True, vmem_limit_bytes=62 * 2**20
        ),
    )(right_side, coupling, face_columns, ghost_lists)


def solution(mesh):
    n_fx, n_fy = mesh.shape["fx"], mesh.shape["fy"]
    low = 1
    while low * low * 4 <= n_fx:
        low *= 2

    def body(right_side, coupling, face_columns, ghost_lists):
        shape = (n_fx, n_fy, low, right_side.shape[0])
        return on_device(shape, right_side, coupling.transpose(1, 0, 2), face_columns, ghost_lists)

    placed = (
        P(("fx", "fy"), None),
        P(("fx", "fy"), None, None),
        P(("fx", "fy"), None),
        P(("fx", "fy"), None),
    )
    return jax.shard_map(
        body,
        mesh=mesh,
        in_specs=placed,
        out_specs=(P(("fx", "fy"), None), P(("fx", "fy"), None)),
        check_vma=False,
    )
```

```python
import functools

import jax
import jax.numpy as jnp
from jax import lax
from jax.experimental import pallas as pl
from jax.experimental.pallas import tpu as pltpu
from jax.sharding import PartitionSpec as P

DOF = 64
NRHS = 32
BLOCKS = 11
OWNED = 7
POWERS = 3
LANES = 128
HALF = DOF // 2
UNROLL = 16
GROUPS = LANES // NRHS
MESH = pl.DeviceIdType.MESH
f32 = jnp.float32
bf16 = jnp.bfloat16


def split(x):
    hi = x.astype(bf16).astype(f32)
    return hi, x - hi


def lane_group(rows):
    return lax.broadcasted_iota(jnp.int32, (rows, LANES), 1) // NRHS


def pick(group, parts):
    out = parts[-1]
    for index in range(len(parts) - 2, -1, -1):
        out = jnp.where(group == index, parts[index], out)
    return out


def replicate(group, rolled, source):
    return pick(group, [rolled[(lane - source) % GROUPS] for lane in range(GROUPS)])


def rolls(x):
    return [x] + [pltpu.roll(x, step * NRHS, 1) for step in range(1, GROUPS)]


def product_tile(x, group):
    hi, lo = split(x)
    zero = jnp.zeros_like(x)
    top = pick(group, [hi, zero, lo, zero])
    bottom = pick(group, [zero, hi, zero, lo])
    return top.astype(bf16), bottom.astype(bf16)


def kernel(shape, right_ref, coupling_ref, columns_ref, ghost_ref, sol_ref, res_ref,
           stage, spread, mats, w0, w1, w2, w3, tiles, acc, send_buf, recv_buf,
           zbuf, vbuf, gram_buf, plane_recv, line_recv, final_buf, wide,
           load_sem, send_sem, recv_sem, ps_sem, pr_sem, ls_sem, lr_sem, as_sem, ar_sem):
    n_fx, n_fy, low, faces = shape
    plane = low * n_fy
    high = n_fx // low
    i = lax.axis_index("fx")
    j = lax.axis_index("fy")
    my_low = i % low
    my_high = i // low
    my_rank = my_low * n_fy + j
    fields = [w0, w1, w2, w3]

    def plane_target(offset):
        rank = lax.rem(my_rank + offset, plane)
        return rank, (my_high * low + rank // n_fy, rank % n_fy)

    def line_target(offset):
        place = lax.rem(my_high + offset, high)
        return (place * low + my_low, j)

    routes = [
        (1, i < n_fx - 1, (i + 1, j), i > 0),
        (0, i > 0, (i - 1, j), i < n_fx - 1),
        (3, j < n_fy - 1, (i, j + 1), j > 0),
        (2, j > 0, (i, j - 1), j < n_fy - 1),
    ]

    loads = [pltpu.make_async_copy(coupling_ref.at[k], stage.at[k], load_sem.at[k]) for k in range(BLOCKS)]
    for load in loads:
        load.start()

    barrier = pltpu.get_barrier_semaphore()
    for _, has_target, target, _ in routes:
        @pl.when(has_target)
        def _(target=target):
            pl.semaphore_signal(barrier, inc=1, device_id=target, device_id_type=MESH)
    for offset in range(1, plane):
        pl.semaphore_signal(barrier, inc=1, device_id=plane_target(offset)[1], device_id_type=MESH)
    for offset in range(1, high):
        pl.semaphore_signal(barrier, inc=1, device_id=line_target(offset), device_id_type=MESH)

    g8 = lane_group(8)
    g64 = lane_group(DOF)
    g32 = lane_group(HALF)

    for block in range(faces // 8):
        for tile in range(DOF // GROUPS):
            x = right_ref[8 * block:8 * block + 8, tile * LANES:(tile + 1) * LANES]
            moved = rolls(x)
            for q in range(GROUPS):
                wide[0, pl.ds(8 * block * DOF + tile * GROUPS + q, 8, stride=DOF), :] = replicate(g8, moved, q)
    for face in range(faces):
        w0[face] = wide[0, face * DOF:(face + 1) * DOF, :]

    def field_copies(power):
        return [
            pltpu.make_async_remote_copy(
                src_ref=send_buf.at[power, q], dst_ref=recv_buf.at[power, q],
                send_sem=send_sem.at[power, q], recv_sem=recv_sem.at[power, q],
                device_id=routes[q][2], device_id_type=MESH,
            )
            for q in range(4)
        ]

    def send_field(power):
        field = fields[power]
        copies = field_copies(power)
        for q, (row, has_target, _, _) in enumerate(routes):
            picked = [field[ghost_ref[row, g]] for g in range(GROUPS)]
            send_buf[power, q] = pick(g64, picked)
        if power == 0:
            count = sum(jnp.where(route[1], 1, 0) for route in routes) + (plane - 1) + (high - 1)
            pl.semaphore_wait(barrier, count)
        for q, (_, has_target, _, _) in enumerate(routes):
            @pl.when(has_target)
            def _(copy=copies[q]):
                copy.start()
        return copies

    def build_own(power):
        field = fields[power]

        @pl.loop(0, faces)
        def _(face):
            x = field[face]
            top, bottom = product_tile(x, g64)
            tiles[face, 0:DOF] = top
            tiles[face, DOF:2 * DOF] = bottom

    def own_products():
        @pl.loop(0, faces // UNROLL)
        def _(part):
            for sub in range(UNROLL):
                face = part * UNROLL + sub
                right = jnp.concatenate([tiles[columns_ref[face, k]] for k in range(OWNED)], axis=0)
                out = jnp.dot(mats[face, :, :OWNED * LANES], right, preferred_element_type=f32)
                acc[face] = out[:HALF] + out[HALF:]

    def far_products(power):
        field = fields[power + 1]

        @pl.loop(0, faces // UNROLL)
        def _(part):
            for sub in range(UNROLL):
                face = part * UNROLL + sub
                right = jnp.concatenate(
                    [tiles[columns_ref[face, k]] for k in range(OWNED, BLOCKS)], axis=0
                )
                out = jnp.dot(mats[face, :, OWNED * LANES:], right, preferred_element_type=f32)
                total = acc[face] + (out[:HALF] + out[HALF:])
                total = total + pltpu.roll(total, LANES // 2, 1)
                turned = pltpu.roll(total, NRHS, 1)
                even = g32 % 2 == 0
                field[face, pl.ds(0, HALF, stride=2), :] = jnp.where(even, total, turned)
                field[face, pl.ds(1, HALF, stride=2), :] = jnp.where(even, turned, total)

    def receive_field(power, copies):
        for q in (2, 3, 0, 1):
            _, has_target, _, has_source = routes[q]

            @pl.when(has_source)
            def _(copy=copies[q]):
                copy.wait_recv()

            @pl.when(jnp.logical_not(has_source))
            def _(q=q):
                recv_buf[power, q] = jnp.zeros((DOF, LANES), f32)
            moved = rolls(recv_buf[power, q])
            for g in range(GROUPS):
                top, bottom = product_tile(replicate(g64, moved, g), g64)
                tiles[faces + q * GROUPS + g, 0:DOF] = top
                tiles[faces + q * GROUPS + g, DOF:2 * DOF] = bottom

            @pl.when(has_target)
            def _(copy=copies[q]):
                copy.wait_send()

    def prepare():
        for k in range(BLOCKS):
            loads[k].wait()
            for block in range(faces // 8):
                for t in range(HALF):
                    spread[k % 2, pl.ds(8 * block * HALF + t, 8, stride=HALF), :] = stage[
                        k, 8 * block:8 * block + 8, t * LANES:(t + 1) * LANES]
            for face in range(faces):
                hi, lo = split(spread[k % 2, face * HALF:(face + 1) * HALF, :])
                mats[face, 0:HALF, k * LANES:(k + 1) * LANES] = hi.astype(bf16)
                mats[face, HALF:DOF, k * LANES:(k + 1) * LANES] = lo.astype(bf16)

    for power in range(POWERS):
        copies = send_field(power)
        build_own(power)
        if power == 0:
            prepare()
        own_products()
        receive_field(power, copies)
        far_products(power)

    @pl.loop(0, faces)
    def _(face):
        rows = pl.ds(pl.multiple_of(face * DOF, DOF), DOF)
        a, b, c, d = [field[face] for field in fields]
        hi, lo = split(pick(g64, [a + b, b + c, c + d, a]))
        zbuf[rows, :LANES] = hi.astype(bf16)
        zbuf[rows, LANES:] = lo.astype(bf16)

    z = zbuf[...]
    both = lax.dot_general(z, z, (((0,), (0,)), ((), ())), preferred_element_type=f32)
    gram = (both[:LANES, :LANES] + both[LANES:, LANES:]) + (both[:LANES, LANES:] + both[LANES:, :LANES])
    share = LANES // plane
    for rank in range(plane):
        gram_buf[rank] = gram[rank * share:(rank + 1) * share]

    copies = []
    for offset in range(1, plane):
        rank, target = plane_target(offset)
        copy = pltpu.make_async_remote_copy(
            src_ref=gram_buf.at[rank], dst_ref=plane_recv.at[offset], send_sem=ps_sem.at[offset],
            recv_sem=pr_sem.at[offset], device_id=target, device_id_type=MESH)
        copy.start()
        copies.append(copy)

    @pl.loop(0, faces)
    def _(face):
        rows = pl.ds(pl.multiple_of(face * DOF, DOF), DOF)
        hi, lo = split(pick(g64, [field[face] for field in fields]))
        vbuf[rows, :LANES] = hi.astype(bf16)
        vbuf[rows, LANES:] = lo.astype(bf16)

    total = gram_buf[my_rank]
    for offset, copy in enumerate(copies, 1):
        copy.wait_recv()
        total = total + plane_recv[offset]
    line_recv[my_high] = total
    line = []
    for offset in range(1, high):
        copy = pltpu.make_async_remote_copy(
            src_ref=line_recv.at[my_high], dst_ref=line_recv.at[my_high], send_sem=ls_sem.at[offset],
            recv_sem=lr_sem.at[offset], device_id=line_target(offset), device_id_type=MESH)
        copy.start()
        line.append(copy)
    for copy in copies:
        copy.wait_send()
    for copy in line:
        copy.wait_recv()
    total = line_recv[0]
    for place in range(1, high):
        total = total + line_recv[place]
    final_buf[my_rank] = total
    gather = []
    for offset in range(1, plane):
        copy = pltpu.make_async_remote_copy(
            src_ref=final_buf.at[my_rank], dst_ref=final_buf.at[my_rank], send_sem=as_sem.at[offset],
            recv_sem=ar_sem.at[offset], device_id=plane_target(offset)[1], device_id_type=MESH)
        copy.start()
        gather.append(copy)
    for copy in line:
        copy.wait_send()
    for copy in gather:
        copy.wait_recv()

    full = jnp.concatenate([final_buf[rank] for rank in range(plane)], axis=0)
    count = POWERS * NRHS
    tiles = [full[8 * t:8 * t + 8] for t in range(count // 8)]
    sub = lax.broadcasted_iota(jnp.int32, (8, LANES), 0)

    def across(x, lane):
        return jnp.broadcast_to(x[:, lane:lane + 1], (8, LANES))

    def down(x, row):
        return jnp.broadcast_to(x[row:row + 1, :], (8, LANES))

    for home in range(len(tiles)):
        mine = tiles[home]
        cols = [across(mine, 8 * home + c) for c in range(8)]
        for step in range(8):
            inverse = 1.0 / down(cols[step], step)
            here = sub == step
            factor = cols[step]
            scaled = down(mine, step) * inverse
            mine = jnp.where(here, scaled, mine - factor * scaled)
            for c in range(step + 1, 8):
                scaled = down(cols[c], step) * inverse
                cols[c] = jnp.where(here, scaled, cols[c] - factor * scaled)
        tiles[home] = mine
        rows8 = [down(mine, c) for c in range(8)]
        order = [t % len(tiles) for t in range(home + 1, home + len(tiles))]
        for t in order:
            terms = [across(tiles[t], 8 * home + c) * rows8[c] for c in range(8)]
            while len(terms) > 1:
                terms = [terms[k] + terms[k + 1] for k in range(0, len(terms), 2)]
            tiles[t] = tiles[t] - terms[0]
    solved = jnp.concatenate(tiles, axis=0)
    coeffs = replicate(lane_group(count), rolls(solved), GROUPS - 1)
    none = jnp.zeros((NRHS, LANES), f32)
    row = lax.broadcasted_iota(jnp.int32, (LANES, LANES), 0)
    col = lax.broadcasted_iota(jnp.int32, (LANES, LANES), 1) % NRHS
    first = jnp.where(row == col, 1.0, 0.0)
    padded = jnp.concatenate([coeffs, none], axis=0)
    combo = first - (padded + jnp.concatenate([none, coeffs], axis=0))
    hi, lo = split(jnp.concatenate([padded, combo], axis=1))
    hi, lo = hi.astype(bf16), lo.astype(bf16)
    twice = jnp.concatenate([hi, hi], axis=0)

    @pl.loop(0, faces // 4)
    def _(quad):
        rows = pl.ds(pl.multiple_of(quad * 4 * DOF, 4 * DOF), 4 * DOF)
        left = vbuf[rows, :]
        out = jnp.dot(left, twice, preferred_element_type=f32)
        wide_part = out + jnp.dot(left[:, :LANES], lo, preferred_element_type=f32)
        wide[0, rows, :] = wide_part[:, :LANES]
        wide[1, rows, :] = wide_part[:, LANES:]
    for part, out_ref in enumerate((sol_ref, res_ref)):
        for block in range(faces // 8):
            for tile in range(DOF // GROUPS):
                parts = [
                    wide[part, pl.ds(8 * block * DOF + tile * GROUPS + q, 8, stride=DOF), :] for q in range(GROUPS)
                ]
                out_ref[8 * block:8 * block + 8, tile * LANES:(tile + 1) * LANES] = pick(g8, parts)
    for copy in gather:
        copy.wait_send()


def on_device(shape, right_side, coupling, face_columns, ghost_lists):
    n_fx, n_fy, low, faces = shape
    plane = low * n_fy
    high = n_fx // low
    share = LANES // plane
    rows = faces * DOF
    vmem = pl.BlockSpec(memory_space=pltpu.VMEM)
    smem = pl.BlockSpec(memory_space=pltpu.SMEM)
    dma = pltpu.SemaphoreType.DMA
    out = jax.ShapeDtypeStruct(right_side.shape, f32)
    return pl.pallas_call(
        functools.partial(kernel, shape),
        out_shape=(out, out),
        in_specs=[vmem, pl.BlockSpec(memory_space=pltpu.HBM), smem, smem],
        out_specs=(vmem, vmem),
        scratch_shapes=[
            pltpu.VMEM(coupling.shape, f32),
            pltpu.VMEM((2, faces * HALF, LANES), f32),
            pltpu.VMEM((faces, DOF, BLOCKS * LANES), bf16),
        ]
        + [pltpu.VMEM((faces, DOF, LANES), f32)] * (POWERS + 1)
        + [
            pltpu.VMEM((faces + 4 * GROUPS, LANES, LANES), bf16),
            pltpu.VMEM((faces, HALF, LANES), f32),
            pltpu.VMEM((POWERS, 4, DOF, LANES), f32),
            pltpu.VMEM((POWERS, 4, DOF, LANES), f32),
            pltpu.VMEM((rows, 2 * LANES), bf16),
            pltpu.VMEM((rows, 2 * LANES), bf16),
            pltpu.VMEM((plane, share, LANES), f32),
            pltpu.VMEM((plane, share, LANES), f32),
            pltpu.VMEM((high, share, LANES), f32),
            pltpu.VMEM((plane, share, LANES), f32),
            pltpu.VMEM((2, rows, LANES), f32),
            dma((BLOCKS,)),
            dma((POWERS, 4)),
            dma((POWERS, 4)),
            dma((plane,)),
            dma((plane,)),
            dma((high,)),
            dma((high,)),
            dma((plane,)),
            dma((plane,)),
        ],
        compiler_params=pltpu.CompilerParams(
            collective_id=0, has_side_effects=True, vmem_limit_bytes=40 * 2**20
        ),
    )(right_side, pltpu.with_memory_space_constraint(coupling, pltpu.HBM), face_columns, ghost_lists)


def solution(mesh):
    n_fx, n_fy = mesh.shape["fx"], mesh.shape["fy"]
    low = 1
    while low * low * 4 <= n_fx:
        low *= 2

    def body(right_side, coupling, face_columns, ghost_lists):
        shape = (n_fx, n_fy, low, right_side.shape[0])
        return on_device(shape, right_side, coupling.transpose(1, 0, 2), face_columns, ghost_lists)

    placed = (
        P(("fx", "fy"), None),
        P(("fx", "fy"), None, None),
        P(("fx", "fy"), None),
        P(("fx", "fy"), None),
    )
    return jax.shard_map(
        body,
        mesh=mesh,
        in_specs=placed,
        out_specs=(P(("fx", "fy"), None), P(("fx", "fy"), None)),
        check_vma=False,
    )
```

```python
import functools

import jax
import jax.numpy as jnp
from jax import lax
from jax.experimental import pallas as pl
from jax.experimental.pallas import tpu as pltpu
from jax.sharding import PartitionSpec as P

DOF = 64
NRHS = 32
BLOCKS = 11
OWNED = 7
POWERS = 3
LANES = 128
HALF = DOF // 2
UNROLL = 16
GROUPS = LANES // NRHS
MESH = pl.DeviceIdType.MESH
f32 = jnp.float32
bf16 = jnp.bfloat16


def split(x):
    hi = x.astype(bf16).astype(f32)
    return hi, x - hi


def lane_group(rows):
    return lax.broadcasted_iota(jnp.int32, (rows, LANES), 1) // NRHS


def pick(group, parts):
    out = parts[-1]
    for index in range(len(parts) - 2, -1, -1):
        out = jnp.where(group == index, parts[index], out)
    return out


def replicate(group, rolled, source):
    return pick(group, [rolled[(lane - source) % GROUPS] for lane in range(GROUPS)])


def rolls(x):
    return [x] + [pltpu.roll(x, step * NRHS, 1) for step in range(1, GROUPS)]


def product_tile(x, group):
    hi, lo = split(x)
    zero = jnp.zeros_like(x)
    top = pick(group, [hi, zero, lo, zero])
    bottom = pick(group, [zero, hi, zero, lo])
    return top.astype(bf16), bottom.astype(bf16)


def kernel(shape, right_ref, coupling_ref, columns_ref, ghost_ref, sol_ref, res_ref,
           stage, spread, mats, w0, w1, w2, w3, tiles, acc, send_buf, recv_buf,
           zbuf, vbuf, gram_buf, plane_recv, line_recv, final_buf, wide,
           load_sem, send_sem, recv_sem, ps_sem, pr_sem, ls_sem, lr_sem, as_sem, ar_sem):
    n_fx, n_fy, low, faces = shape
    plane = low * n_fy
    high = n_fx // low
    i = lax.axis_index("fx")
    j = lax.axis_index("fy")
    my_low = i % low
    my_high = i // low
    my_rank = my_low * n_fy + j
    fields = [w0, w1, w2, w3]

    def plane_target(offset):
        rank = lax.rem(my_rank + offset, plane)
        return rank, (my_high * low + rank // n_fy, rank % n_fy)

    def line_target(offset):
        place = lax.rem(my_high + offset, high)
        return (place * low + my_low, j)

    routes = [
        (1, i < n_fx - 1, (i + 1, j), i > 0),
        (0, i > 0, (i - 1, j), i < n_fx - 1),
        (3, j < n_fy - 1, (i, j + 1), j > 0),
        (2, j > 0, (i, j - 1), j < n_fy - 1),
    ]

    loads = [pltpu.make_async_copy(coupling_ref.at[k], stage.at[k], load_sem.at[k]) for k in range(BLOCKS)]
    for load in loads:
        load.start()

    barrier = pltpu.get_barrier_semaphore()
    for _, has_target, target, _ in routes:
        @pl.when(has_target)
        def _(target=target):
            pl.semaphore_signal(barrier, inc=1, device_id=target, device_id_type=MESH)
    for offset in range(1, plane):
        pl.semaphore_signal(barrier, inc=1, device_id=plane_target(offset)[1], device_id_type=MESH)
    for offset in range(1, high):
        pl.semaphore_signal(barrier, inc=1, device_id=line_target(offset), device_id_type=MESH)

    g8 = lane_group(8)
    g64 = lane_group(DOF)
    g32 = lane_group(HALF)

    for block in range(faces // 8):
        for tile in range(DOF // GROUPS):
            x = right_ref[8 * block:8 * block + 8, tile * LANES:(tile + 1) * LANES]
            moved = rolls(x)
            for q in range(GROUPS):
                wide[0, pl.ds(8 * block * DOF + tile * GROUPS + q, 8, stride=DOF), :] = replicate(g8, moved, q)
    for face in range(faces):
        w0[face] = wide[0, face * DOF:(face + 1) * DOF, :]

    def field_copies(power):
        return [
            pltpu.make_async_remote_copy(
                src_ref=send_buf.at[power, q], dst_ref=recv_buf.at[power, q],
                send_sem=send_sem.at[power, q], recv_sem=recv_sem.at[power, q],
                device_id=routes[q][2], device_id_type=MESH,
            )
            for q in range(4)
        ]

    def send_field(power):
        field = fields[power]
        copies = field_copies(power)
        for q, (row, has_target, _, _) in enumerate(routes):
            picked = [field[ghost_ref[row, g]] for g in range(GROUPS)]
            send_buf[power, q] = pick(g64, picked)
            if power == 0 and q == 0:
                count = sum(jnp.where(route[1], 1, 0) for route in routes) + (plane - 1) + (high - 1)
                pl.semaphore_wait(barrier, count)

            @pl.when(has_target)
            def _(copy=copies[q]):
                copy.start()
        return copies

    def build_own(power):
        field = fields[power]

        @pl.loop(0, faces, unroll=4)
        def _(face):
            x = field[face]
            top, bottom = product_tile(x, g64)
            tiles[face, 0:DOF] = top
            tiles[face, DOF:2 * DOF] = bottom

    def own_products():
        @pl.loop(0, faces // UNROLL)
        def _(part):
            for sub in range(UNROLL):
                face = part * UNROLL + sub
                right = jnp.concatenate([tiles[columns_ref[face, k]] for k in range(OWNED)], axis=0)
                out = jnp.dot(mats[face, :, :OWNED * LANES], right, preferred_element_type=f32)
                acc[face] = out[:HALF] + out[HALF:]

    def far_products(power):
        field = fields[power + 1]

        @pl.loop(0, faces // UNROLL)
        def _(part):
            for sub in range(UNROLL):
                face = part * UNROLL + sub
                right = jnp.concatenate(
                    [tiles[columns_ref[face, k]] for k in range(OWNED, BLOCKS)], axis=0
                )
                out = jnp.dot(mats[face, :, OWNED * LANES:], right, preferred_element_type=f32)
                total = acc[face] + (out[:HALF] + out[HALF:])
                total = total + pltpu.roll(total, LANES // 2, 1)
                turned = pltpu.roll(total, NRHS, 1)
                even = g32 % 2 == 0
                field[face, pl.ds(0, HALF, stride=2), :] = jnp.where(even, total, turned)
                field[face, pl.ds(1, HALF, stride=2), :] = jnp.where(even, turned, total)

    def receive_field(power, copies):
        for q in (2, 3, 0, 1):
            _, has_target, _, has_source = routes[q]

            @pl.when(has_source)
            def _(copy=copies[q]):
                copy.wait_recv()

            @pl.when(jnp.logical_not(has_source))
            def _(q=q):
                recv_buf[power, q] = jnp.zeros((DOF, LANES), f32)
            moved = rolls(recv_buf[power, q])
            for g in range(GROUPS):
                top, bottom = product_tile(replicate(g64, moved, g), g64)
                tiles[faces + q * GROUPS + g, 0:DOF] = top
                tiles[faces + q * GROUPS + g, DOF:2 * DOF] = bottom

            @pl.when(has_target)
            def _(copy=copies[q]):
                copy.wait_send()

    def prepare():
        for k in range(BLOCKS):
            loads[k].wait()
            for block in range(faces // 8):
                for t in range(HALF):
                    spread[k % 2, pl.ds(8 * block * HALF + t, 8, stride=HALF), :] = stage[
                        k, 8 * block:8 * block + 8, t * LANES:(t + 1) * LANES]
            for face in range(faces):
                hi, lo = split(spread[k % 2, face * HALF:(face + 1) * HALF, :])
                mats[face, 0:HALF, k * LANES:(k + 1) * LANES] = hi.astype(bf16)
                mats[face, HALF:DOF, k * LANES:(k + 1) * LANES] = lo.astype(bf16)

    for power in range(POWERS):
        copies = send_field(power)
        build_own(power)
        if power == 0:
            prepare()
        own_products()
        receive_field(power, copies)
        far_products(power)

    @pl.loop(0, faces, unroll=4)
    def _(face):
        rows = pl.ds(pl.multiple_of(face * DOF, DOF), DOF)
        a, b, c, d = [field[face] for field in fields]
        hi, lo = split(pick(g64, [a + b, b + c, c + d, a]))
        zbuf[rows, :LANES] = hi.astype(bf16)
        zbuf[rows, LANES:] = lo.astype(bf16)

    z = zbuf[...]
    both = lax.dot_general(z, z, (((0,), (0,)), ((), ())), preferred_element_type=f32)
    gram = (both[:LANES, :LANES] + both[LANES:, LANES:]) + (both[:LANES, LANES:] + both[LANES:, :LANES])
    share = LANES // plane
    for rank in range(plane):
        gram_buf[rank] = gram[rank * share:(rank + 1) * share]

    copies = []
    for offset in range(1, plane):
        rank, target = plane_target(offset)
        copy = pltpu.make_async_remote_copy(
            src_ref=gram_buf.at[rank], dst_ref=plane_recv.at[offset], send_sem=ps_sem.at[offset],
            recv_sem=pr_sem.at[offset], device_id=target, device_id_type=MESH)
        copy.start()
        copies.append(copy)

    @pl.loop(0, faces, unroll=4)
    def _(face):
        rows = pl.ds(pl.multiple_of(face * DOF, DOF), DOF)
        hi, lo = split(pick(g64, [field[face] for field in fields]))
        vbuf[rows, :LANES] = hi.astype(bf16)
        vbuf[rows, LANES:] = lo.astype(bf16)

    total = gram_buf[my_rank]
    for offset, copy in enumerate(copies, 1):
        copy.wait_recv()
        total = total + plane_recv[offset]
    line_recv[my_high] = total
    line = []
    for offset in range(1, high):
        copy = pltpu.make_async_remote_copy(
            src_ref=line_recv.at[my_high], dst_ref=line_recv.at[my_high], send_sem=ls_sem.at[offset],
            recv_sem=lr_sem.at[offset], device_id=line_target(offset), device_id_type=MESH)
        copy.start()
        line.append(copy)
    for copy in copies:
        copy.wait_send()
    for copy in line:
        copy.wait_recv()
    total = line_recv[0]
    for place in range(1, high):
        total = total + line_recv[place]
    final_buf[my_rank] = total
    gather = []
    for offset in range(1, plane):
        copy = pltpu.make_async_remote_copy(
            src_ref=final_buf.at[my_rank], dst_ref=final_buf.at[my_rank], send_sem=as_sem.at[offset],
            recv_sem=ar_sem.at[offset], device_id=plane_target(offset)[1], device_id_type=MESH)
        copy.start()
        gather.append(copy)
    for copy in line:
        copy.wait_send()
    for copy in gather:
        copy.wait_recv()

    full = jnp.concatenate([final_buf[rank] for rank in range(plane)], axis=0)
    count = POWERS * NRHS
    tiles = [full[8 * t:8 * t + 8] for t in range(count // 8)]
    sub = lax.broadcasted_iota(jnp.int32, (8, LANES), 0)

    def across(x, lane):
        return jnp.broadcast_to(x[:, lane:lane + 1], (8, LANES))

    def down(x, row):
        return jnp.broadcast_to(x[row:row + 1, :], (8, LANES))

    for home in range(len(tiles)):
        mine = tiles[home]
        cols = [across(mine, 8 * home + c) for c in range(8)]
        for step in range(8):
            inverse = 1.0 / down(cols[step], step)
            here = sub == step
            factor = cols[step]
            scaled = down(mine, step) * inverse
            mine = jnp.where(here, scaled, mine - factor * scaled)
            for c in range(step + 1, 8):
                scaled = down(cols[c], step) * inverse
                cols[c] = jnp.where(here, scaled, cols[c] - factor * scaled)
        tiles[home] = mine
        rows8 = [down(mine, c) for c in range(8)]
        order = [t % len(tiles) for t in range(home + 1, home + len(tiles))]
        for t in order:
            terms = [across(tiles[t], 8 * home + c) * rows8[c] for c in range(8)]
            while len(terms) > 1:
                terms = [terms[k] + terms[k + 1] for k in range(0, len(terms), 2)]
            tiles[t] = tiles[t] - terms[0]
    solved = jnp.concatenate(tiles, axis=0)
    coeffs = replicate(lane_group(count), rolls(solved), GROUPS - 1)
    none = jnp.zeros((NRHS, LANES), f32)
    row = lax.broadcasted_iota(jnp.int32, (LANES, LANES), 0)
    col = lax.broadcasted_iota(jnp.int32, (LANES, LANES), 1) % NRHS
    first = jnp.where(row == col, 1.0, 0.0)
    padded = jnp.concatenate([coeffs, none], axis=0)
    combo = first - (padded + jnp.concatenate([none, coeffs], axis=0))
    hi, lo = split(jnp.concatenate([padded, combo], axis=1))
    hi, lo = hi.astype(bf16), lo.astype(bf16)
    twice = jnp.concatenate([hi, hi], axis=0)

    @pl.loop(0, faces // 4, unroll=True)
    def _(quad):
        rows = pl.ds(pl.multiple_of(quad * 4 * DOF, 4 * DOF), 4 * DOF)
        left = vbuf[rows, :]
        out = jnp.dot(left, twice, preferred_element_type=f32)
        wide_part = out + jnp.dot(left[:, :LANES], lo, preferred_element_type=f32)
        wide[0, rows, :] = wide_part[:, :LANES]
        wide[1, rows, :] = wide_part[:, LANES:]
    for part, out_ref in enumerate((sol_ref, res_ref)):
        for block in range(faces // 8):
            for tile in range(DOF // GROUPS):
                parts = [
                    wide[part, pl.ds(8 * block * DOF + tile * GROUPS + q, 8, stride=DOF), :] for q in range(GROUPS)
                ]
                out_ref[8 * block:8 * block + 8, tile * LANES:(tile + 1) * LANES] = pick(g8, parts)
    for copy in gather:
        copy.wait_send()


def on_device(shape, right_side, coupling, face_columns, ghost_lists):
    n_fx, n_fy, low, faces = shape
    plane = low * n_fy
    high = n_fx // low
    share = LANES // plane
    rows = faces * DOF
    vmem = pl.BlockSpec(memory_space=pltpu.VMEM)
    smem = pl.BlockSpec(memory_space=pltpu.SMEM)
    dma = pltpu.SemaphoreType.DMA
    out = jax.ShapeDtypeStruct(right_side.shape, f32)
    return pl.pallas_call(
        functools.partial(kernel, shape),
        out_shape=(out, out),
        in_specs=[vmem, pl.BlockSpec(memory_space=pltpu.HBM), smem, smem],
        out_specs=(vmem, vmem),
        scratch_shapes=[
            pltpu.VMEM(coupling.shape, f32),
            pltpu.VMEM((2, faces * HALF, LANES), f32),
            pltpu.VMEM((faces, DOF, BLOCKS * LANES), bf16),
        ]
        + [pltpu.VMEM((faces, DOF, LANES), f32)] * (POWERS + 1)
        + [
            pltpu.VMEM((faces + 4 * GROUPS, LANES, LANES), bf16),
            pltpu.VMEM((faces, HALF, LANES), f32),
            pltpu.VMEM((POWERS, 4, DOF, LANES), f32),
            pltpu.VMEM((POWERS, 4, DOF, LANES), f32),
            pltpu.VMEM((rows, 2 * LANES), bf16),
            pltpu.VMEM((rows, 2 * LANES), bf16),
            pltpu.VMEM((plane, share, LANES), f32),
            pltpu.VMEM((plane, share, LANES), f32),
            pltpu.VMEM((high, share, LANES), f32),
            pltpu.VMEM((plane, share, LANES), f32),
            pltpu.VMEM((2, rows, LANES), f32),
            dma((BLOCKS,)),
            dma((POWERS, 4)),
            dma((POWERS, 4)),
            dma((plane,)),
            dma((plane,)),
            dma((high,)),
            dma((high,)),
            dma((plane,)),
            dma((plane,)),
        ],
        compiler_params=pltpu.CompilerParams(
            collective_id=0, has_side_effects=True, vmem_limit_bytes=40 * 2**20
        ),
    )(right_side, pltpu.with_memory_space_constraint(coupling, pltpu.HBM), face_columns, ghost_lists)


def solution(mesh):
    n_fx, n_fy = mesh.shape["fx"], mesh.shape["fy"]
    low = 1
    while low * low * 4 <= n_fx:
        low *= 2

    def body(right_side, coupling, face_columns, ghost_lists):
        shape = (n_fx, n_fy, low, right_side.shape[0])
        return on_device(shape, right_side, coupling.transpose(1, 0, 2), face_columns, ghost_lists)

    placed = (
        P(("fx", "fy"), None),
        P(("fx", "fy"), None, None),
        P(("fx", "fy"), None),
        P(("fx", "fy"), None),
    )
    return jax.shard_map(
        body,
        mesh=mesh,
        in_specs=placed,
        out_specs=(P(("fx", "fy"), None), P(("fx", "fy"), None)),
        check_vma=False,
    )
```
